32 devices in a mesh: expert: 2 (over y), hidden: 4 (over z), dp: 4 (over x, core).
Axes of the slice: x: 2, y: 2, z: 4, core: 2. Of those that a mesh axis runs over, the one named last changes fastest.
Arguments:
- tokens: bfloat16 [2, 4, 512, 2048], P('expert', 'dp', None, 'hidden'), may hold values from -6 to 6
- grad_out: bfloat16 [2, 4, 512, 2048], P('expert', 'dp', None, 'hidden'), may hold values from -0.25 to 0.25
- gate_weight: bfloat16 [4, 2048, 512], P('expert', 'dp', 'hidden'), may hold values from -0.125 to 0.125
- up_weight: bfloat16 [4, 2048, 512], P('expert', 'dp', 'hidden'), may hold values from -0.125 to 0.125
- down_weight: bfloat16 [4, 512, 2048], P('expert', 'hidden', 'dp'), may hold values from -0.25 to 0.25
- matching: int32 [2], replicated, may hold values from 0 to 1, each once
- block_counts: int32 [2, 4, 2], P('expert', 'dp'), may hold values from 0 to 4, as said below
Outputs:
- grad_gate: bfloat16 [4, 2048, 512], P('expert', 'dp', 'hidden')
- grad_up: bfloat16 [4, 2048, 512], P('expert', 'dp', 'hidden')
- grad_down: bfloat16 [4, 512, 2048], P('expert', 'hidden', 'dp')
The draws below stay inside these ranges and needn't reach their ends.
Inputs may be any that keep to these rules, and one draw needn't show every extreme that they name: `matching`: each expert index appears once. `block_counts`: the 2 counts of one expert index and data index sum to at most 4; on some device one count equals 4.
All inputs are finite; a program needn't handle non-finite values.
Results may differ from the reference program's by a relative error of at most 0.008.
Values may be sent and summed in bfloat16 or wider, within the bound.
A program may use at most 64 MiB of HBM per device.

```python
import jax
import jax.numpy as jnp
from jax import lax

D = 2048
HID = 512
EXP_DEV = 2
BLOCK = 128
BLOCKS = 4
ROWS = 512
EXPERTS = 4
N_EXPERT = 2
N_DP = 4


def draw_block_counts(key, part):
    folded = jax.random.fold_in(key, 11)
    key_total, key_cut, key_pick, key_expert = jax.random.split(folded, 4)
    totals = jax.random.randint(key_total, (N_EXPERT, N_DP), BLOCKS // 2, BLOCKS + 1)
    cut_points = jax.random.randint(key_cut, (N_EXPERT, N_DP, EXP_DEV - 1), 0, BLOCKS + 1)
    cut_points = jnp.sort(jnp.minimum(cut_points, totals[:, :, None]), axis=2)
    boundary = jnp.concatenate([jnp.zeros((N_EXPERT, N_DP, 1), jnp.int32), cut_points.astype(jnp.int32), totals[:, :, None].astype(jnp.int32)], axis=2)
    counts = boundary[:, :, 1:] - boundary[:, :, :-1]
    chosen = jax.random.randint(key_pick, (), 0, N_EXPERT * N_DP)
    expert = jax.random.randint(key_expert, (), 0, EXP_DEV)
    whole_load = (jnp.arange(EXP_DEV) == expert).astype(jnp.int32) * BLOCKS
    stacked = counts.reshape(N_EXPERT * N_DP, EXP_DEV)
    stacked = jnp.where((jnp.arange(N_EXPERT * N_DP) == chosen)[:, None], whole_load[None, :], stacked)
    return stacked.reshape(N_EXPERT, N_DP, EXP_DEV).astype(jnp.int32)


def shard_levels(rng, dims, shards, smallest, high):
    def one(position, shards_of):
        steps = jax.random.uniform(jax.random.fold_in(jax.random.fold_in(rng, 6), position), (shards_of,), jnp.float32, smallest / len(shards), high / len(shards))
        return jnp.repeat(jnp.exp(steps), dims[position] // shards_of).reshape((-1,) + (1,) * (len(dims) - position - 1))

    loudness = one(*shards[0])
    for cut in shards[1:]:
        loudness = loudness * one(*cut)
    return loudness


def centred(stream_key, shape, deviation, reach, cuts=(), kind=jnp.bfloat16):
    entries = deviation * jax.random.normal(stream_key, shape, jnp.float32)
    if cuts:
        entries = entries * shard_levels(stream_key, shape, cuts, -0.22, 0.18)
    return jnp.clip(entries, -reach, reach).astype(kind)


def setup_inputs(seed: int = 0) -> dict:
    splits = jax.random.split(jax.random.key(seed), 8)
    return {
        "tokens": centred(splits[0], (N_EXPERT, N_DP, ROWS, D), 1.0, 6.0, ((0, 2), (1, 4), (3, 4))),
        "grad_out": centred(splits[1], (N_EXPERT, N_DP, ROWS, D), (2.0 / (N_DP * ROWS) ** 0.5), 0.25, ((0, 2), (1, 4), (3, 4))),
        "gate_weight": centred(splits[2], (EXPERTS, D, HID), D ** -0.5, 0.125, ((0, 2), (1, 4), (2, 4))),
        "up_weight": centred(splits[3], (EXPERTS, D, HID), D ** -0.5, 0.125, ((0, 2), (1, 4), (2, 4))),
        "down_weight": centred(splits[4], (EXPERTS, HID, D), HID ** -0.5, 0.25, ((0, 2), (1, 4), (2, 4))),
        "matching": jax.random.permutation(splits[5], N_EXPERT).astype(jnp.int32),
        "block_counts": draw_block_counts(jax.random.fold_in(splits[7], 71), 0),
    }


def contract_rows(left, right):
    return lax.dot_general(left, right, (((0,), (0,)), ((), ())), preferred_element_type=jnp.float32)


def block_owners(counts, blocks):
    bounds = jnp.cumsum(counts).astype(jnp.int32)
    index = jnp.arange(blocks, dtype=jnp.int32)
    owner = jnp.sum((index[:, None] >= bounds[None, :]).astype(jnp.int32), axis=1)
    owner = jnp.minimum(owner, counts.shape[0] - 1).astype(jnp.int32)
    alive = (index < bounds[-1]).astype(jnp.float32)
    return owner, alive


def add_into(total, term, expert):
    current = lax.dynamic_index_in_dim(total, expert, 0, keepdims=True)
    return lax.dynamic_update_index_in_dim(total, current + term[None], expert, 0)


def expert_terms(row_blocks, grad_blocks, weight_gate, weight_up, weight_down, owner, alive):
    zeros_gate = jnp.zeros(weight_gate.shape, jnp.float32)
    zeros_down = jnp.zeros(weight_down.shape, jnp.float32)

    def step(carry, inputs):
        total_gate, total_up, total_down = carry
        row_block, grad_block, expert, live = inputs
        gate_matrix = lax.dynamic_index_in_dim(weight_gate, expert, 0, keepdims=False)
        up_matrix = lax.dynamic_index_in_dim(weight_up, expert, 0, keepdims=False)
        down_matrix = lax.dynamic_index_in_dim(weight_down, expert, 0, keepdims=False)
        gate_value = jnp.dot(row_block, gate_matrix, preferred_element_type=jnp.float32)
        up_value = jnp.dot(row_block, up_matrix, preferred_element_type=jnp.float32)
        sigmoid_gate = jax.nn.sigmoid(gate_value)
        activated = gate_value * sigmoid_gate
        hidden = (activated * up_value * live).astype(jnp.bfloat16)
        grad_hidden = lax.dot_general(grad_block, down_matrix, (((1,), (1,)), ((), ())), preferred_element_type=jnp.float32)
        grad_gate = (grad_hidden * up_value * sigmoid_gate * (1.0 + gate_value * (1.0 - sigmoid_gate)) * live).astype(jnp.bfloat16)
        grad_up = (grad_hidden * activated * live).astype(jnp.bfloat16)
        total_gate = add_into(total_gate, contract_rows(row_block, grad_gate), expert)
        total_up = add_into(total_up, contract_rows(row_block, grad_up), expert)
        total_down = add_into(total_down, contract_rows(hidden, grad_block), expert)
        return (total_gate, total_up, total_down), None

    totals, unused = lax.scan(step, (zeros_gate, zeros_gate, zeros_down), (row_blocks, grad_blocks, owner, alive))
    return totals


def reference(tokens, grad_out, gate_weight, up_weight, down_weight, matching, block_counts):
    blocks = ROWS // BLOCK

    def per_slot(inputs):
        slot_tokens, slot_grads, slot_counts, source = inputs
        start = (source * EXP_DEV).astype(jnp.int32)
        weight_gate = lax.dynamic_slice_in_dim(gate_weight, start, EXP_DEV, 0)
        weight_up = lax.dynamic_slice_in_dim(up_weight, start, EXP_DEV, 0)
        weight_down = lax.dynamic_slice_in_dim(down_weight, start, EXP_DEV, 0)
        sums = None
        for data_index in range(N_DP):
            owner, alive = block_owners(slot_counts[data_index], blocks)
            row_blocks = slot_tokens[data_index].reshape(blocks, BLOCK, D)
            grad_blocks = slot_grads[data_index].reshape(blocks, BLOCK, D)
            terms = expert_terms(row_blocks, grad_blocks, weight_gate, weight_up, weight_down, owner, alive)
            rounded = tuple(lax.optimization_barrier(term.astype(jnp.bfloat16)).astype(jnp.float32) for term in terms)
            if sums is None:
                sums = rounded
            else:
                sums = tuple(left + right for left, right in zip(sums, rounded))
        return tuple(total.astype(jnp.bfloat16) for total in sums)

    moved = lax.map(per_slot, (tokens, grad_out, block_counts, matching))
    grad_gate = moved[0].reshape(EXPERTS, D, HID)
    grad_up = moved[1].reshape(EXPERTS, D, HID)
    grad_down = moved[2].reshape(EXPERTS, HID, D)
    return (grad_gate, grad_up, grad_down)
```

```python
import functools

import jax
import jax.numpy as jnp
from jax import lax
from jax.experimental import pallas as pl
from jax.experimental.pallas import tpu as pltpu
from jax.sharding import PartitionSpec as P

BLOCK = 128


def contract_rows(left, right):
    return lax.dot_general(
        left, right, (((0,), (0,)), ((), ())), preferred_element_type=jnp.float32
    )


def block_owners(counts, blocks):
    bounds = jnp.cumsum(counts)
    index = jnp.arange(blocks, dtype=jnp.int32)
    owner = jnp.sum((index[:, None] >= bounds[None, :]).astype(jnp.int32), axis=1)
    owner = jnp.minimum(owner, counts.shape[0] - 1)
    alive = (index < bounds[-1]).astype(jnp.float32)
    return (owner, alive)


def add_into(total, term, expert):
    current = lax.dynamic_index_in_dim(total, expert, 0, keepdims=True)
    return lax.dynamic_update_index_in_dim(total, current + term[None], expert, 0)


def expert_terms(row_blocks, grad_blocks, weight_gate, weight_up, weight_down, owner, alive):
    zeros_gate = jnp.zeros(weight_gate.shape, jnp.float32)
    zeros_down = jnp.zeros(weight_down.shape, jnp.float32)

    def step(carry, inputs):
        total_gate, total_up, total_down = carry
        row_block, grad_block, expert, live = inputs
        gate_matrix = lax.dynamic_index_in_dim(weight_gate, expert, 0, keepdims=False)
        up_matrix = lax.dynamic_index_in_dim(weight_up, expert, 0, keepdims=False)
        down_matrix = lax.dynamic_index_in_dim(weight_down, expert, 0, keepdims=False)
        gate_value = jnp.dot(row_block, gate_matrix, preferred_element_type=jnp.float32)
        up_value = jnp.dot(row_block, up_matrix, preferred_element_type=jnp.float32)
        sigmoid_gate = jax.nn.sigmoid(gate_value)
        activated = gate_value * sigmoid_gate
        hidden = (activated * up_value * live).astype(jnp.bfloat16)
        grad_hidden = lax.dot_general(
            grad_block, down_matrix, (((1,), (1,)), ((), ())), preferred_element_type=jnp.float32
        )
        grad_gate = (
            grad_hidden * up_value * sigmoid_gate * (1.0 + gate_value * (1.0 - sigmoid_gate)) * live
        ).astype(jnp.bfloat16)
        grad_up = (grad_hidden * activated * live).astype(jnp.bfloat16)
        total_gate = add_into(total_gate, contract_rows(row_block, grad_gate), expert)
        total_up = add_into(total_up, contract_rows(row_block, grad_up), expert)
        total_down = add_into(total_down, contract_rows(hidden, grad_block), expert)
        return ((total_gate, total_up, total_down), None)

    totals, unused = lax.scan(
        step, (zeros_gate, zeros_gate, zeros_down), (row_blocks, grad_blocks, owner, alive)
    )
    return totals


def relocate(arrays, matching):
    groups = lax.axis_size("expert")
    joined = jnp.concatenate([array_piece.reshape(groups, -1) for array_piece in arrays], axis=1)
    spread = lax.all_to_all(joined, "expert", split_axis=0, concat_axis=0, tiled=True)
    ordered = jnp.take(spread, matching, axis=0)
    settled = lax.all_to_all(ordered, "expert", split_axis=0, concat_axis=0, tiled=True)
    pieces = []
    offset = 0
    for array_piece in arrays:
        length = array_piece.size // groups
        pieces.append(settled[:, offset : offset + length].reshape(array_piece.shape))
        offset = offset + length
    return pieces


def on_device_plain(tokens, grad_out, gate_weight, up_weight, down_weight, matching, block_counts):
    moved = relocate((gate_weight, up_weight, down_weight), matching)
    weight_gate, weight_up, weight_down = (
        lax.all_gather(moved[0], "dp", axis=1, tiled=True),
        lax.all_gather(moved[1], "dp", axis=1, tiled=True),
        lax.all_gather(moved[2], "dp", axis=2, tiled=True),
    )
    rows_full, grads_full = (
        lax.all_gather(tokens[0, 0], "hidden", axis=1, tiled=True),
        lax.all_gather(grad_out[0, 0], "hidden", axis=1, tiled=True),
    )
    blocks = rows_full.shape[0] // BLOCK
    width = rows_full.shape[1]
    owner, alive = block_owners(block_counts[0, 0], blocks)
    totals = expert_terms(
        rows_full.reshape(blocks, BLOCK, width),
        grads_full.reshape(blocks, BLOCK, width),
        weight_gate,
        weight_up,
        weight_down,
        owner,
        alive,
    )
    summed = (
        lax.psum_scatter(
            totals[0].astype(jnp.bfloat16), "dp", scatter_dimension=1, tiled=True
        ).astype(jnp.float32),
        lax.psum_scatter(
            totals[1].astype(jnp.bfloat16), "dp", scatter_dimension=1, tiled=True
        ).astype(jnp.float32),
        lax.psum_scatter(
            totals[2].astype(jnp.bfloat16), "dp", scatter_dimension=2, tiled=True
        ).astype(jnp.float32),
    )
    return (
        summed[0].astype(jnp.bfloat16),
        summed[1].astype(jnp.bfloat16),
        summed[2].astype(jnp.bfloat16),
    )


MESH = pl.DeviceIdType.MESH
TILE = 256


def flip(index, bit):
    return index + bit - 2 * bit * ((index // bit) % 2)


def fused_kernel(
    exchange, experts, counts_ref, match_ref, tok_ref, grad_ref, gate_ref, up_ref, down_ref,
    out_gate, out_up, out_down,
    tok_all, grad_all, gu_all, dn_all, old_gate, old_up, old_down,
    acc_gu, acc_gh, pre, hid, gate_sel, up_sel,
    part_gu, part_dn, core_gu, core_dn, sum_gu, sum_dn, far_gu, far_dn,
    z_send, z_recv, y_send, y_recv, w_send, w_recv, r_send, r_recv,
):
    zs = lax.axis_size("hidden")
    h = lax.axis_index("hidden")
    d = lax.axis_index("dp")
    p = lax.axis_index("expert")
    rows, feats = tok_ref.shape
    width = gate_ref.shape[2]
    blocks = rows // BLOCK
    near, far = flip(d, 1), flip(d, 2)
    cross = flip(near, 2)

    def remote(source, target, send, recv, where):
        return pltpu.make_async_remote_copy(
            src_ref=source, dst_ref=target, send_sem=send, recv_sem=recv,
            device_id=where, device_id_type=MESH,
        )

    barrier = pltpu.get_barrier_semaphore()
    for bit_partner in (near, far):
        pl.semaphore_signal(barrier, inc=1, device_id={"dp": bit_partner}, device_id_type=MESH)
    if exchange:
        pl.semaphore_signal(barrier, inc=1, device_id={"expert": 1 - p}, device_id_type=MESH)

    @pl.when(h > 0)
    def _():
        pl.semaphore_signal(barrier, inc=1, device_id={"hidden": h - 1}, device_id_type=MESH)

    @pl.when(h < zs - 1)
    def _():
        pl.semaphore_signal(barrier, inc=1, device_id={"hidden": h + 1}, device_id_type=MESH)

    peers = (h + zs - 1) // zs + (2 * zs - 2 - h) // zs
    pl.semaphore_wait(barrier, peers + (3 if exchange else 2))

    mine = (tok_ref, grad_ref)
    whole = (tok_all, grad_all)

    def line(kind, way, step, slab):
        to = h + 1 if way == 0 else h - 1
        source = mine[kind] if step == 0 else whole[kind].at[slab]
        return remote(
            source, whole[kind].at[slab], z_send.at[kind, way, step], z_recv.at[kind, way, step],
            {"hidden": to},
        )

    def sends(way, step):
        if way == 0:
            return (h + 1 < zs) & (h - step >= 0), h - step
        return (h - 1 >= 0) & (h + step < zs), h + step

    def takes(way, step):
        if way == 0:
            return h - 1 - step >= 0, h - 1 - step
        return h + 1 + step < zs, h + 1 + step

    def line_start(kind, step):
        for way in (0, 1):
            valid, slab = sends(way, step)

            @pl.when(valid)
            def _():
                line(kind, way, step, slab).start()

    def line_finish(kind, step):
        for way in (0, 1):
            valid, slab = sends(way, step)

            @pl.when(valid)
            def _():
                line(kind, way, step, slab).wait_send()

    def line_take(kind, step):
        for way in (0, 1):
            valid, slab = takes(way, step)

            @pl.when(valid)
            def _():
                line(kind, way, step, slab).wait_recv()
        if step + 1 < zs - 1:
            line_start(kind, step + 1)

    def swap(i):
        source = (gate_ref, up_ref, down_ref)[i]
        target = (old_gate, old_up, old_down)[i]
        return remote(source, target, y_send.at[i], y_recv.at[i], {"expert": 1 - p})

    line_start(0, 0)
    if exchange:
        swap(0).start()
        swap(1).start()
    line_start(1, 0)
    if exchange:
        swap(2).start()

    tok_all[h] = tok_ref[...]
    grad_all[h] = grad_ref[...]

    def chosen(own, other, e):
        if not exchange:
            return own[e]
        return jnp.where(match_ref[p] == p, own[e], other[e])

    weights = (gu_all, dn_all)

    def spread(kind, i):
        slab = (d, d, far)[i]
        to = (far, near, near)[i]
        ref = weights[kind].at[slab]
        return remote(ref, ref, w_send.at[kind, i], w_recv.at[kind, i], {"dp": to})

    def arrived(kind, i):
        slab = (far, near, cross)[i]
        ref = weights[kind].at[slab]
        remote(ref, ref, w_send.at[kind, i], w_recv.at[kind, i], {"dp": near}).wait_recv()

    if exchange:
        swap(0).wait_recv()
        swap(1).wait_recv()
    for e in range(experts):
        gu_all[d, e, :, :width] = chosen(gate_ref, old_gate, e)
        gu_all[d, e, :, width:] = chosen(up_ref, old_up, e)
    spread(0, 0).start()
    spread(0, 1).start()
    line_take(0, 0)
    if exchange:
        swap(2).wait_recv()
    for e in range(experts):
        dn_all[d, e * width : (e + 1) * width, :] = chosen(down_ref, old_down, e)
    spread(1, 0).start()
    spread(1, 1).start()
    line_take(1, 0)
    for kind in (0, 1):
        arrived(kind, 0)
        spread(kind, 2).start()
    for kind in (0, 1):
        arrived(kind, 1)
        arrived(kind, 2)

    def add_tokens(slab, first=False):
        @pl.loop(0, rows // TILE)
        def _(i):
            part = pl.ds(pl.multiple_of(i * TILE, TILE), TILE)
            for e in range(experts):
                term = jnp.dot(tok_all[slab, part], gu_all[slab, e], preferred_element_type=jnp.float32)
                acc_gu[e, part] = term if first else acc_gu[e, part] + term

    def add_grads(slab, first=False):
        @pl.loop(0, rows // TILE)
        def _(i):
            part = pl.ds(pl.multiple_of(i * TILE, TILE), TILE)
            term = lax.dot_general(
                grad_all[slab, part], dn_all[slab], (((1,), (1,)), ((), ())),
                preferred_element_type=jnp.float32,
            )
            acc_gh[part] = term if first else acc_gh[part] + term

    def add_step(kind, step):
        for way in (0, 1):
            valid, slab = takes(way, step)

            @pl.when(valid)
            def _():
                (add_tokens, add_grads)[kind](slab)

    add_tokens(h, True)
    add_grads(h, True)
    add_step(0, 0)
    add_step(1, 0)
    for step in range(1, zs - 2):
        line_take(0, step)
        add_step(0, step)
        line_take(1, step)
        add_step(1, step)
    line_take(0, zs - 2)
    add_step(0, zs - 2)

    bounds = [counts_ref[0]]
    for e in range(1, experts):
        bounds.append(bounds[-1] + counts_ref[e])
    picks, masks = [], []
    for b in range(blocks):
        owner = jnp.int32(0)
        for e in range(experts):
            owner = owner + jnp.where(b >= bounds[e], 1, 0)
        owner = jnp.minimum(owner, experts - 1)
        alive = jnp.where(b < bounds[-1], 1.0, 0.0)
        picks.append([jnp.where(owner == e, 1.0, 0.0) for e in range(experts)])
        masks.append([picks[b][e] * alive for e in range(experts)])

    for b in range(blocks):
        part = slice(b * BLOCK, (b + 1) * BLOCK)
        both = sum(acc_gu[e, part] * picks[b][e] for e in range(experts))
        gate_value, up_value = both[:, :width], both[:, width:]
        gate_sel[part] = gate_value
        up_sel[part] = up_value
        hidden = (gate_value * jax.nn.sigmoid(gate_value) * up_value)
        for e in range(experts):
            hid[part, e * width : (e + 1) * width] = (hidden * masks[b][e]).astype(jnp.bfloat16)

    line_take(1, zs - 2)
    add_step(1, zs - 2)

    def reduce_near(kind, i):
        slab = (cross, near)[i]
        source = (part_gu, part_dn)[kind].at[slab]
        target = (core_gu, core_dn)[kind].at[i]
        return remote(source, target, r_send.at[kind, i], r_recv.at[kind, i], {"dp": near})

    def reduce_far(kind):
        return remote(
            (sum_gu, sum_dn)[kind], (far_gu, far_dn)[kind], r_send.at[kind, 2], r_recv.at[kind, 2],
            {"dp": far},
        )

    def down_term(slab):
        part_dn[slab] = lax.dot_general(
            hid[...], grad_all[slab], (((0,), (0,)), ((), ())), preferred_element_type=jnp.float32
        ).astype(jnp.bfloat16)

    def gate_term(slab):
        @pl.loop(0, feats // TILE)
        def _(i):
            part = pl.ds(pl.multiple_of(i * TILE, TILE), TILE)
            part_gu[slab, part] = lax.dot_general(
                tok_all[slab, :, part], pre[...], (((0,), (0,)), ((), ())),
                preferred_element_type=jnp.float32,
            ).astype(jnp.bfloat16)

    def add_near(kind, i, slab):
        own = (part_gu, part_dn)[kind]
        got = (core_gu, core_dn)[kind]
        return own[slab].astype(jnp.float32) + got[i].astype(jnp.float32)

    def down_first():
        down_term(cross)
        reduce_near(1, 0).start()
        down_term(far)
        reduce_near(1, 0).wait_recv()
        sum_dn[...] = add_near(1, 0, far).astype(jnp.bfloat16)
        reduce_far(1).start()

    def down_rest():
        down_term(near)
        reduce_near(1, 1).start()
        down_term(d)

    for b in range(blocks):
        part = slice(b * BLOCK, (b + 1) * BLOCK)
        gate_value, up_value = gate_sel[part], up_sel[part]
        grad_hidden = sum(
            acc_gh[part, e * width : (e + 1) * width] * picks[b][e] for e in range(experts)
        )
        s = jax.nn.sigmoid(gate_value)
        grad_gate = grad_hidden * up_value * s * (1.0 + gate_value * (1.0 - s))
        grad_up = grad_hidden * gate_value * s
        for e in range(experts):
            at = e * 2 * width
            pre[part, at : at + width] = (grad_gate * masks[b][e]).astype(jnp.bfloat16)
            pre[part, at + width : at + 2 * width] = (grad_up * masks[b][e]).astype(jnp.bfloat16)

    gate_term(cross)
    reduce_near(0, 0).start()
    gate_term(far)
    reduce_near(0, 0).wait_recv()
    sum_gu[...] = add_near(0, 0, far).astype(jnp.bfloat16)
    reduce_far(0).start()
    down_first()
    gate_term(near)
    reduce_near(0, 1).start()
    gate_term(d)
    down_rest()

    reduce_near(0, 1).wait_recv()
    reduce_far(0).wait_recv()
    total = add_near(0, 1, d) + far_gu[...].astype(jnp.float32)
    for e in range(experts):
        at = e * 2 * width
        out_gate[e] = total[:, at : at + width].astype(jnp.bfloat16)
        out_up[e] = total[:, at + width : at + 2 * width].astype(jnp.bfloat16)
    reduce_near(1, 1).wait_recv()
    reduce_far(1).wait_recv()
    total = add_near(1, 1, d) + far_dn[...].astype(jnp.float32)
    for e in range(experts):
        out_down[e] = total[e * width : (e + 1) * width].astype(jnp.bfloat16)

    for kind in (0, 1):
        for step in range(zs - 1):
            line_finish(kind, step)
        for i in range(3):
            spread(kind, i).wait_send()
        for i in range(2):
            reduce_near(kind, i).wait_send()
        reduce_far(kind).wait_send()
    if exchange:
        for i in range(3):
            swap(i).wait_send()


def on_device_fused(tokens, grad_out, gate_weight, up_weight, down_weight, matching, block_counts):
    groups = lax.axis_size("expert")
    zs = lax.axis_size("hidden")
    ds = lax.axis_size("dp")
    exchange = groups == 2
    if not exchange:
        gate_weight, up_weight, down_weight = relocate(
            (gate_weight, up_weight, down_weight), matching
        )
        matching = jnp.zeros_like(matching)
    rows, feats = tokens.shape[2:]
    experts, part, width = gate_weight.shape
    vmem = pl.BlockSpec(memory_space=pltpu.VMEM)
    smem = pl.BlockSpec(memory_space=pltpu.SMEM)
    half, full = jnp.bfloat16, jnp.float32
    wide = experts * 2 * width
    tall = experts * width
    dma = pltpu.SemaphoreType.DMA
    return pl.pallas_call(
        functools.partial(fused_kernel, exchange, experts),
        out_shape=tuple(
            jax.ShapeDtypeStruct(w.shape, half) for w in (gate_weight, up_weight, down_weight)
        ),
        in_specs=[smem, smem] + [vmem] * 5,
        out_specs=(vmem,) * 3,
        scratch_shapes=[
            pltpu.VMEM((zs, rows, feats), half),
            pltpu.VMEM((zs, rows, feats), half),
            pltpu.VMEM((ds, experts, part, 2 * width), half),
            pltpu.VMEM((ds, tall, part), half),
            pltpu.VMEM(gate_weight.shape, half),
            pltpu.VMEM(up_weight.shape, half),
            pltpu.VMEM(down_weight.shape, half),
            pltpu.VMEM((experts, rows, 2 * width), full),
            pltpu.VMEM((rows, tall), full),
            pltpu.VMEM((rows, wide), half),
            pltpu.VMEM((rows, tall), half),
            pltpu.VMEM((rows, width), full),
            pltpu.VMEM((rows, width), full),
            pltpu.VMEM((ds, part, wide), half),
            pltpu.VMEM((ds, tall, part), half),
            pltpu.VMEM((2, part, wide), half),
            pltpu.VMEM((2, tall, part), half),
            pltpu.VMEM((part, wide), half),
            pltpu.VMEM((tall, part), half),
            pltpu.VMEM((part, wide), half),
            pltpu.VMEM((tall, part), half),
            dma((2, 2, zs - 1)),
            dma((2, 2, zs - 1)),
            dma((3,)),
            dma((3,)),
            dma((2, 3)),
            dma((2, 3)),
            dma((2, 3)),
            dma((2, 3)),
        ],
        compiler_params=pltpu.CompilerParams(
            collective_id=0, has_side_effects=True, vmem_limit_bytes=48 * 1024 * 1024
        ),
    )(
        block_counts.reshape(-1), matching, tokens.reshape(rows, feats),
        grad_out.reshape(rows, feats), gate_weight, up_weight, down_weight,
    )


def fused_fits(mesh):
    return mesh.shape["dp"] == 4 and mesh.shape["hidden"] == 4


def solution(mesh):
    on_device = on_device_fused if fused_fits(mesh) else on_device_plain
    in_specs = (
        P("expert", "dp", None, "hidden"),
        P("expert", "dp", None, "hidden"),
        P("expert", "dp", "hidden"),
        P("expert", "dp", "hidden"),
        P("expert", "hidden", "dp"),
        P(),
        P("expert", "dp", None),
    )
    out_specs = (
        P("expert", "dp", "hidden"),
        P("expert", "dp", "hidden"),
        P("expert", "hidden", "dp"),
    )
    return jax.shard_map(
        on_device, mesh=mesh, in_specs=in_specs, out_specs=out_specs, check_vma=False
    )
```

```python
import functools

import jax
import jax.numpy as jnp
from jax import lax
from jax.experimental import pallas as pl
from jax.experimental.pallas import tpu as pltpu
from jax.sharding import PartitionSpec as P

BLOCK = 128


def contract_rows(left, right):
    return lax.dot_general(
        left, right, (((0,), (0,)), ((), ())), preferred_element_type=jnp.float32
    )


def block_owners(counts, blocks):
    bounds = jnp.cumsum(counts)
    index = jnp.arange(blocks, dtype=jnp.int32)
    owner = jnp.sum((index[:, None] >= bounds[None, :]).astype(jnp.int32), axis=1)
    owner = jnp.minimum(owner, counts.shape[0] - 1)
    alive = (index < bounds[-1]).astype(jnp.float32)
    return (owner, alive)


def add_into(total, term, expert):
    current = lax.dynamic_index_in_dim(total, expert, 0, keepdims=True)
    return lax.dynamic_update_index_in_dim(total, current + term[None], expert, 0)


def expert_terms(row_blocks, grad_blocks, weight_gate, weight_up, weight_down, owner, alive):
    zeros_gate = jnp.zeros(weight_gate.shape, jnp.float32)
    zeros_down = jnp.zeros(weight_down.shape, jnp.float32)

    def step(carry, inputs):
        total_gate, total_up, total_down = carry
        row_block, grad_block, expert, live = inputs
        gate_matrix = lax.dynamic_index_in_dim(weight_gate, expert, 0, keepdims=False)
        up_matrix = lax.dynamic_index_in_dim(weight_up, expert, 0, keepdims=False)
        down_matrix = lax.dynamic_index_in_dim(weight_down, expert, 0, keepdims=False)
        gate_value = jnp.dot(row_block, gate_matrix, preferred_element_type=jnp.float32)
        up_value = jnp.dot(row_block, up_matrix, preferred_element_type=jnp.float32)
        sigmoid_gate = jax.nn.sigmoid(gate_value)
        activated = gate_value * sigmoid_gate
        hidden = (activated * up_value * live).astype(jnp.bfloat16)
        grad_hidden = lax.dot_general(
            grad_block, down_matrix, (((1,), (1,)), ((), ())), preferred_element_type=jnp.float32
        )
        grad_gate = (
            grad_hidden * up_value * sigmoid_gate * (1.0 + gate_value * (1.0 - sigmoid_gate)) * live
        ).astype(jnp.bfloat16)
        grad_up = (grad_hidden * activated * live).astype(jnp.bfloat16)
        total_gate = add_into(total_gate, contract_rows(row_block, grad_gate), expert)
        total_up = add_into(total_up, contract_rows(row_block, grad_up), expert)
        total_down = add_into(total_down, contract_rows(hidden, grad_block), expert)
        return ((total_gate, total_up, total_down), None)

    totals, unused = lax.scan(
        step, (zeros_gate, zeros_gate, zeros_down), (row_blocks, grad_blocks, owner, alive)
    )
    return totals


def relocate(arrays, matching):
    groups = lax.axis_size("expert")
    joined = jnp.concatenate([array_piece.reshape(groups, -1) for array_piece in arrays], axis=1)
    spread = lax.all_to_all(joined, "expert", split_axis=0, concat_axis=0, tiled=True)
    ordered = jnp.take(spread, matching, axis=0)
    settled = lax.all_to_all(ordered, "expert", split_axis=0, concat_axis=0, tiled=True)
    pieces = []
    offset = 0
    for array_piece in arrays:
        length = array_piece.size // groups
        pieces.append(settled[:, offset : offset + length].reshape(array_piece.shape))
        offset = offset + length
    return pieces


def on_device_plain(tokens, grad_out, gate_weight, up_weight, down_weight, matching, block_counts):
    moved = relocate((gate_weight, up_weight, down_weight), matching)
    weight_gate, weight_up, weight_down = (
        lax.all_gather(moved[0], "dp", axis=1, tiled=True),
        lax.all_gather(moved[1], "dp", axis=1, tiled=True),
        lax.all_gather(moved[2], "dp", axis=2, tiled=True),
    )
    rows_full, grads_full = (
        lax.all_gather(tokens[0, 0], "hidden", axis=1, tiled=True),
        lax.all_gather(grad_out[0, 0], "hidden", axis=1, tiled=True),
    )
    blocks = rows_full.shape[0] // BLOCK
    width = rows_full.shape[1]
    owner, alive = block_owners(block_counts[0, 0], blocks)
    totals = expert_terms(
        rows_full.reshape(blocks, BLOCK, width),
        grads_full.reshape(blocks, BLOCK, width),
        weight_gate,
        weight_up,
        weight_down,
        owner,
        alive,
    )
    summed = (
        lax.psum_scatter(
            totals[0].astype(jnp.bfloat16), "dp", scatter_dimension=1, tiled=True
        ).astype(jnp.float32),
        lax.psum_scatter(
            totals[1].astype(jnp.bfloat16), "dp", scatter_dimension=1, tiled=True
        ).astype(jnp.float32),
        lax.psum_scatter(
            totals[2].astype(jnp.bfloat16), "dp", scatter_dimension=2, tiled=True
        ).astype(jnp.float32),
    )
    return (
        summed[0].astype(jnp.bfloat16),
        summed[1].astype(jnp.bfloat16),
        summed[2].astype(jnp.bfloat16),
    )


MESH = pl.DeviceIdType.MESH
TILE = 256


def flip(index, bit):
    return index + bit - 2 * bit * ((index // bit) % 2)


def fused_kernel(
    exchange, experts, counts_ref, match_ref, tok_ref, grad_ref, gate_ref, up_ref, down_ref,
    out_gate, out_up, out_down,
    tok_all, grad_all, gu_all, dn_all, own_gate, own_up, own_down, old_gate, old_up, old_down,
    acc_gu, acc_gh, pre, hid, gate_sel, up_sel,
    part_gu, part_dn, core_gu, core_dn, sum_gu, sum_dn, far_gu, far_dn,
    dn_end, hid_out, hid_in, hid_end, acc_end, gh_out, gh_in,
    part_de, core_de, sum_de, far_de, done_de, got_de,
    z_send, z_recv, y_send, y_recv, w_send, w_recv, r_send, r_recv, e_send, e_recv, l_sem,
):
    zs = lax.axis_size("hidden")
    h = lax.axis_index("hidden")
    d = lax.axis_index("dp")
    p = lax.axis_index("expert")
    rows, feats = tok_ref.shape
    width = gate_ref.shape[2]
    blocks = rows // BLOCK
    near, far = flip(d, 1), flip(d, 2)
    cross = flip(near, 2)
    middle = (h > 0) & (h < zs - 1)
    border = (h == 0) | (h == zs - 1)
    helper = 1 + (h // (zs - 1)) * (zs - 3)
    end = (h - 1) * (zs - 1)
    last = (zs - 2 - h) * (zs - 1)

    def remote(source, target, send, recv, where):
        return pltpu.make_async_remote_copy(
            src_ref=source, dst_ref=target, send_sem=send, recv_sem=recv,
            device_id=where, device_id_type=MESH,
        )

    barrier = pltpu.get_barrier_semaphore()
    for bit_partner in (near, far):
        pl.semaphore_signal(barrier, inc=1, device_id={"dp": bit_partner}, device_id_type=MESH)
    if exchange:
        pl.semaphore_signal(barrier, inc=1, device_id={"expert": 1 - p}, device_id_type=MESH)

    @pl.when(h > 0)
    def _():
        pl.semaphore_signal(barrier, inc=1, device_id={"hidden": h - 1}, device_id_type=MESH)

    @pl.when(h < zs - 1)
    def _():
        pl.semaphore_signal(barrier, inc=1, device_id={"hidden": h + 1}, device_id_type=MESH)

    peers = (h + zs - 1) // zs + (2 * zs - 2 - h) // zs
    pl.semaphore_wait(barrier, peers + (3 if exchange else 2))

    mine = (tok_ref, grad_ref)
    whole = (tok_all, grad_all)

    def line(kind, way, step, slab):
        to = h + 1 if way == 0 else h - 1
        source = mine[kind] if step == 0 else whole[kind].at[slab]
        return remote(
            source, whole[kind].at[slab], z_send.at[kind, way, step], z_recv.at[kind, way, step],
            {"hidden": to},
        )

    def sends(kind, way, step):
        if way == 0:
            return (h + 1 < zs - kind) & (h - step >= 0), h - step
        return (h - 1 >= kind) & (h + step < zs), h + step

    def takes(kind, way, step):
        if way == 0:
            valid, slab = h - 1 - step >= 0, h - 1 - step
        else:
            valid, slab = h + 1 + step < zs, h + 1 + step
        return (valid & middle) if kind else valid, slab

    def line_start(kind, step, ways=(0, 1)):
        for way in ways:
            valid, slab = sends(kind, way, step)

            @pl.when(valid)
            def _():
                line(kind, way, step, slab).start()

    def line_finish(kind, step):
        for way in (0, 1):
            valid, slab = sends(kind, way, step)

            @pl.when(valid)
            def _():
                line(kind, way, step, slab).wait_send()

    def line_take(kind, step, ways=(0, 1)):
        for way in ways:
            valid, slab = takes(kind, way, step)

            @pl.when(valid)
            def _():
                line(kind, way, step, slab).wait_recv()
        if step + 1 < zs - 1:
            line_start(kind, step + 1, ways)

    def swap(i):
        source = (gate_ref, up_ref, down_ref)[i]
        target = (old_gate, old_up, old_down)[i]
        return remote(source, target, y_send.at[i], y_recv.at[i], {"expert": 1 - p})

    line_start(0, 0)
    if exchange:
        for i in range(3):
            swap(i).start()
    local = [
        pltpu.make_async_copy(source, target, l_sem.at[i])
        for i, (source, target) in enumerate((
            (gate_ref, own_gate), (up_ref, own_up), (down_ref, own_down),
            (tok_ref, tok_all.at[h]), (grad_ref, grad_all.at[h]),
        ))
    ]
    for copy in local:
        copy.start()

    def chosen(own, other, e):
        if not exchange:
            return own[e]
        return jnp.where(match_ref[p] == p, own[e], other[e])

    weights = (gu_all, dn_all)

    def spread(kind, i):
        slab = (d, d, far)[i]
        to = (far, near, near)[i]
        ref = weights[kind].at[slab]
        return remote(ref, ref, w_send.at[kind, i], w_recv.at[kind, i], {"dp": to})

    def arrived(kind, i):
        slab = (far, near, cross)[i]
        ref = weights[kind].at[slab]
        remote(ref, ref, w_send.at[kind, i], w_recv.at[kind, i], {"dp": near}).wait_recv()

    line_take(0, 0)
    line_start(1, 0)
    for copy in local:
        copy.wait()
    if exchange:
        swap(0).wait_recv()
        swap(1).wait_recv()
    for e in range(experts):
        gu_all[d, e, :, :width] = chosen(own_gate, old_gate, e)
        gu_all[d, e, :, width:] = chosen(own_up, old_up, e)
    spread(0, 0).start()
    spread(0, 1).start()
    if exchange:
        swap(2).wait_recv()
    for e in range(experts):
        dn_all[d, e * width : (e + 1) * width, :] = chosen(own_down, old_down, e)
    spread(1, 0).start()
    spread(1, 1).start()
    line_take(0, 1)

    @pl.when(h == 1)
    def _():
        line(1, 0, 0, h - 1).wait_recv()
        line(1, 0, 1, h - 1).start()

    @pl.when(h == zs - 2)
    def _():
        line(1, 1, 0, h + 1).wait_recv()
        line(1, 1, 1, h + 1).start()

    for kind in (0, 1):
        arrived(kind, 0)
        spread(kind, 2).start()
    for kind in (0, 1):
        arrived(kind, 1)
        arrived(kind, 2)

    def lend(i, owner, to):
        slab = owner + (i + 1) * (1 - 2 * (owner // (zs - 1)))
        return remote(
            dn_all.at[slab], dn_end.at[slab], e_send.at[i], e_recv.at[i], {"hidden": to}
        )

    hidden_out = remote(hid_out, hid_in, e_send.at[3], e_recv.at[3], {"hidden": helper})
    grads_out = remote(gh_out, gh_in, e_send.at[4], e_recv.at[4], {"hidden": end})
    down_out = remote(done_de, got_de, e_send.at[5], e_recv.at[5], {"hidden": end})

    @pl.when(border)
    def _():
        for i in range(3):
            lend(i, h, helper).start()

    def add_tokens(slab, first=False):
        @pl.loop(0, rows // TILE)
        def _(i):
            part = pl.ds(pl.multiple_of(i * TILE, TILE), TILE)
            for e in range(experts):
                term = jnp.dot(tok_all[slab, part], gu_all[slab, e], preferred_element_type=jnp.float32)
                acc_gu[e, part] = term if first else acc_gu[e, part] + term

    def add_grads(slab, first=False, total=acc_gh, weight=dn_all):
        @pl.loop(0, rows // TILE)
        def _(i):
            part = pl.ds(pl.multiple_of(i * TILE, TILE), TILE)
            term = lax.dot_general(
                grad_all[slab, part], weight[slab], (((1,), (1,)), ((), ())),
                preferred_element_type=jnp.float32,
            )
            total[part] = term if first else total[part] + term

    def add_step(step):
        for way in (0, 1):
            valid, slab = takes(0, way, step)

            @pl.when(valid)
            def _():
                add_tokens(slab)

    add_tokens(h, True)
    add_grads(h, True)
    add_step(0)
    add_step(1)
    line_take(0, zs - 2)
    add_step(zs - 2)

    bounds = [counts_ref[0]]
    for e in range(1, experts):
        bounds.append(bounds[-1] + counts_ref[e])
    picks, masks = [], []
    for b in range(blocks):
        owner = jnp.int32(0)
        for e in range(experts):
            owner = owner + jnp.where(b >= bounds[e], 1, 0)
        owner = jnp.minimum(owner, experts - 1)
        alive = jnp.where(b < bounds[-1], 1.0, 0.0)
        picks.append([jnp.where(owner == e, 1.0, 0.0) for e in range(experts)])
        masks.append([picks[b][e] * alive for e in range(experts)])

    for b in range(blocks):
        part = slice(b * BLOCK, (b + 1) * BLOCK)
        both = sum(acc_gu[e, part] * picks[b][e] for e in range(experts))
        gate_value, up_value = both[:, :width], both[:, width:]
        gate_sel[part] = gate_value
        up_sel[part] = up_value
        hidden = gate_value * jax.nn.sigmoid(gate_value) * up_value
        hid_out[part] = (hidden * sum(masks[b])).astype(jnp.bfloat16)
        for e in range(experts):
            hid[part, e * width : (e + 1) * width] = (hidden * masks[b][e]).astype(jnp.bfloat16)

    @pl.when(border)
    def _():
        hidden_out.start()

    parts = (part_gu, part_dn, part_de)
    cores = (core_gu, core_dn, core_de)
    sums = (sum_gu, sum_dn, sum_de)
    fars = (far_gu, far_dn, far_de)

    def reduce_near(kind, i):
        slab = (cross, near)[i]
        return remote(
            parts[kind].at[slab], cores[kind].at[i], r_send.at[kind, i], r_recv.at[kind, i],
            {"dp": near},
        )

    def reduce_far(kind):
        return remote(
            sums[kind], fars[kind], r_send.at[kind, 2], r_recv.at[kind, 2], {"dp": far}
        )

    def down_term(kind, slab):
        left = hid if kind == 1 else hid_end
        parts[kind][slab] = lax.dot_general(
            left[...], grad_all[slab], (((0,), (0,)), ((), ())), preferred_element_type=jnp.float32
        ).astype(jnp.bfloat16)

    def gate_term(slab):
        @pl.loop(0, feats // TILE)
        def _(i):
            part = pl.ds(pl.multiple_of(i * TILE, TILE), TILE)
            part_gu[slab, part] = lax.dot_general(
                tok_all[slab, :, part], pre[...], (((0,), (0,)), ((), ())),
                preferred_element_type=jnp.float32,
            ).astype(jnp.bfloat16)

    def add_near(kind, i, slab):
        return parts[kind][slab].astype(jnp.float32) + cores[kind][i].astype(jnp.float32)

    def down_phase(kind, late):
        def at_turn(slab):
            return pl.when(slab == last if late else slab != last)

        @at_turn(cross)
        def _():
            down_term(kind, cross)
            reduce_near(kind, 0).start()

        @at_turn(far)
        def _():
            down_term(kind, far)
            reduce_near(kind, 0).wait_recv()
            sums[kind][...] = add_near(kind, 0, far).astype(jnp.bfloat16)
            reduce_far(kind).start()

        @at_turn(near)
        def _():
            down_term(kind, near)
            reduce_near(kind, 1).start()

        @at_turn(d)
        def _():
            down_term(kind, d)

    @pl.when(middle)
    def _():
        @pl.when(h == 1)
        def _():
            line(1, 1, 0, h + 1).wait_recv()

        @pl.when(h == zs - 2)
        def _():
            line(1, 0, 0, h - 1).wait_recv()

        add_grads(h - 1)
        add_grads(h + 1)
        down_phase(1, False)
        for i in range(3):
            lend(i, end, helper).wait_recv()
        add_grads(h, True, acc_end, dn_end)
        add_grads(zs - 1 - h, False, acc_end, dn_end)
        hidden_out.wait_recv()
        for b in range(blocks):
            part = slice(b * BLOCK, (b + 1) * BLOCK)
            value = hid_in[part].astype(jnp.float32)
            for e in range(experts):
                hid_end[part, e * width : (e + 1) * width] = (value * masks[b][e]).astype(
                    jnp.bfloat16
                )
        down_phase(2, False)

        @pl.when(h == 1)
        def _():
            line(1, 1, 1, h + 2).wait_recv()

        @pl.when(h == zs - 2)
        def _():
            line(1, 0, 1, h - 2).wait_recv()

        add_grads(last, False, acc_end, dn_end)
        for b in range(blocks):
            part = slice(b * BLOCK, (b + 1) * BLOCK)
            gh_out[part] = sum(
                acc_end[part, e * width : (e + 1) * width] * picks[b][e] for e in range(experts)
            ).astype(jnp.bfloat16)
        grads_out.start()
        add_grads(last)
        gh_in[...] = jnp.zeros_like(gh_in)

    @pl.when(border)
    def _():
        grads_out.wait_recv()

    for b in range(blocks):
        part = slice(b * BLOCK, (b + 1) * BLOCK)
        gate_value, up_value = gate_sel[part], up_sel[part]
        grad_hidden = sum(
            acc_gh[part, e * width : (e + 1) * width] * picks[b][e] for e in range(experts)
        ) + gh_in[part].astype(jnp.float32)
        s = jax.nn.sigmoid(gate_value)
        grad_gate = grad_hidden * up_value * s * (1.0 + gate_value * (1.0 - s))
        grad_up = grad_hidden * gate_value * s
        for e in range(experts):
            at = e * 2 * width
            pre[part, at : at + width] = (grad_gate * masks[b][e]).astype(jnp.bfloat16)
            pre[part, at + width : at + 2 * width] = (grad_up * masks[b][e]).astype(jnp.bfloat16)

    gate_term(cross)
    reduce_near(0, 0).start()
    gate_term(far)
    reduce_near(0, 0).wait_recv()
    sum_gu[...] = add_near(0, 0, far).astype(jnp.bfloat16)
    reduce_far(0).start()
    gate_term(near)
    reduce_near(0, 1).start()

    @pl.when(middle)
    def _():
        down_phase(2, True)
        down_phase(1, True)

    gate_term(d)

    @pl.when(middle)
    def _():
        reduce_near(2, 1).wait_recv()
        reduce_far(2).wait_recv()
        total = add_near(2, 1, d) + far_de[...].astype(jnp.float32)
        done_de[...] = total.astype(jnp.bfloat16)
        down_out.start()

    reduce_near(0, 1).wait_recv()
    reduce_far(0).wait_recv()
    total = add_near(0, 1, d) + far_gu[...].astype(jnp.float32)
    for e in range(experts):
        at = e * 2 * width
        out_gate[e] = total[:, at : at + width].astype(jnp.bfloat16)
        out_up[e] = total[:, at + width : at + 2 * width].astype(jnp.bfloat16)

    @pl.when(middle)
    def _():
        reduce_near(1, 1).wait_recv()
        reduce_far(1).wait_recv()
        total = add_near(1, 1, d) + far_dn[...].astype(jnp.float32)
        for e in range(experts):
            out_down[e] = total[e * width : (e + 1) * width].astype(jnp.bfloat16)

    @pl.when(border)
    def _():
        down_out.wait_recv()
        for e in range(experts):
            out_down[e] = got_de[e * width : (e + 1) * width]

    def sent(kind):
        for i in range(2):
            reduce_near(kind, i).wait_send()
        reduce_far(kind).wait_send()

    for kind in (0, 1):
        for step in range(zs - 1):
            line_finish(kind, step)
        for i in range(3):
            spread(kind, i).wait_send()
    sent(0)

    @pl.when(middle)
    def _():
        sent(1)
        sent(2)
        grads_out.wait_send()
        down_out.wait_send()

    @pl.when(border)
    def _():
        for i in range(3):
            lend(i, h, helper).wait_send()
        hidden_out.wait_send()

    if exchange:
        for i in range(3):
            swap(i).wait_send()


def on_device_fused(tokens, grad_out, gate_weight, up_weight, down_weight, matching, block_counts):
    groups = lax.axis_size("expert")
    zs = lax.axis_size("hidden")
    ds = lax.axis_size("dp")
    exchange = groups == 2
    if not exchange:
        gate_weight, up_weight, down_weight = relocate(
            (gate_weight, up_weight, down_weight), matching
        )
        matching = jnp.zeros_like(matching)
    rows, feats = tokens.shape[2:]
    experts, part, width = gate_weight.shape
    vmem = pl.BlockSpec(memory_space=pltpu.VMEM)
    smem = pl.BlockSpec(memory_space=pltpu.SMEM)
    half, full = jnp.bfloat16, jnp.float32
    wide = experts * 2 * width
    tall = experts * width
    dma = pltpu.SemaphoreType.DMA
    return pl.pallas_call(
        functools.partial(fused_kernel, exchange, experts),
        out_shape=tuple(
            jax.ShapeDtypeStruct(w.shape, half) for w in (gate_weight, up_weight, down_weight)
        ),
        in_specs=[smem, smem] + [pl.BlockSpec(memory_space=pltpu.HBM)] * 5,
        out_specs=(vmem,) * 3,
        scratch_shapes=[
            pltpu.VMEM((zs, rows, feats), half),
            pltpu.VMEM((zs, rows, feats), half),
            pltpu.VMEM((ds, experts, part, 2 * width), half),
            pltpu.VMEM((ds, tall, part), half),
            pltpu.VMEM(gate_weight.shape, half),
            pltpu.VMEM(up_weight.shape, half),
            pltpu.VMEM(down_weight.shape, half),
            pltpu.VMEM(gate_weight.shape, half),
            pltpu.VMEM(up_weight.shape, half),
            pltpu.VMEM(down_weight.shape, half),
            pltpu.VMEM((experts, rows, 2 * width), full),
            pltpu.VMEM((rows, tall), full),
            pltpu.VMEM((rows, wide), half),
            pltpu.VMEM((rows, tall), half),
            pltpu.VMEM((rows, width), full),
            pltpu.VMEM((rows, width), full),
            pltpu.VMEM((ds, part, wide), half),
            pltpu.VMEM((ds, tall, part), half),
            pltpu.VMEM((2, part, wide), half),
            pltpu.VMEM((2, tall, part), half),
            pltpu.VMEM((part, wide), half),
            pltpu.VMEM((tall, part), half),
            pltpu.VMEM((part, wide), half),
            pltpu.VMEM((tall, part), half),
            pltpu.VMEM((ds, tall, part), half),
            pltpu.VMEM((rows, width), half),
            pltpu.VMEM((rows, width), half),
            pltpu.VMEM((rows, tall), half),
            pltpu.VMEM((rows, tall), full),
            pltpu.VMEM((rows, width), half),
            pltpu.VMEM((rows, width), half),
            pltpu.VMEM((ds, tall, part), half),
            pltpu.VMEM((2, tall, part), half),
            pltpu.VMEM((tall, part), half),
            pltpu.VMEM((tall, part), half),
            pltpu.VMEM((tall, part), half),
            pltpu.VMEM((tall, part), half),
            dma((2, 2, zs - 1)),
            dma((2, 2, zs - 1)),
            dma((3,)),
            dma((3,)),
            dma((2, 3)),
            dma((2, 3)),
            dma((3, 3)),
            dma((3, 3)),
            dma((6,)),
            dma((6,)),
            dma((5,)),
        ],
        compiler_params=pltpu.CompilerParams(
            collective_id=0, has_side_effects=True, vmem_limit_bytes=63 * 1024 * 1024
        ),
    )(
        block_counts.reshape(-1), matching, tokens.reshape(rows, feats),
        grad_out.reshape(rows, feats), gate_weight, up_weight, down_weight,
    )


def fused_fits(mesh):
    return mesh.shape["dp"] == 4 and mesh.shape["hidden"] == 4


def solution(mesh):
    on_device = on_device_fused if fused_fits(mesh) else on_device_plain
    in_specs = (
        P("expert", "dp", None, "hidden"),
        P("expert", "dp", None, "hidden"),
        P("expert", "dp", "hidden"),
        P("expert", "dp", "hidden"),
        P("expert", "hidden", "dp"),
        P(),
        P("expert", "dp", None),
    )
    out_specs = (
        P("expert", "dp", "hidden"),
        P("expert", "dp", "hidden"),
        P("expert", "hidden", "dp"),
    )
    return jax.shard_map(
        on_device, mesh=mesh, in_specs=in_specs, out_specs=out_specs, check_vma=False
    )
```

```python
import functools

import jax
import jax.numpy as jnp
from jax import lax
from jax.experimental import pallas as pl
from jax.experimental.pallas import tpu as pltpu
from jax.sharding import PartitionSpec as P

BLOCK = 128


def contract_rows(left, right):
    return lax.dot_general(
        left, right, (((0,), (0,)), ((), ())), preferred_element_type=jnp.float32
    )


def block_owners(counts, blocks):
    bounds = jnp.cumsum(counts)
    index = jnp.arange(blocks, dtype=jnp.int32)
    owner = jnp.sum((index[:, None] >= bounds[None, :]).astype(jnp.int32), axis=1)
    owner = jnp.minimum(owner, counts.shape[0] - 1)
    alive = (index < bounds[-1]).astype(jnp.float32)
    return (owner, alive)


def add_into(total, term, expert):
    current = lax.dynamic_index_in_dim(total, expert, 0, keepdims=True)
    return lax.dynamic_update_index_in_dim(total, current + term[None], expert, 0)


def expert_terms(row_blocks, grad_blocks, weight_gate, weight_up, weight_down, owner, alive):
    zeros_gate = jnp.zeros(weight_gate.shape, jnp.float32)
    zeros_down = jnp.zeros(weight_down.shape, jnp.float32)

    def step(carry, inputs):
        total_gate, total_up, total_down = carry
        row_block, grad_block, expert, live = inputs
        gate_matrix = lax.dynamic_index_in_dim(weight_gate, expert, 0, keepdims=False)
        up_matrix = lax.dynamic_index_in_dim(weight_up, expert, 0, keepdims=False)
        down_matrix = lax.dynamic_index_in_dim(weight_down, expert, 0, keepdims=False)
        gate_value = jnp.dot(row_block, gate_matrix, preferred_element_type=jnp.float32)
        up_value = jnp.dot(row_block, up_matrix, preferred_element_type=jnp.float32)
        sigmoid_gate = jax.nn.sigmoid(gate_value)
        activated = gate_value * sigmoid_gate
        hidden = (activated * up_value * live).astype(jnp.bfloat16)
        grad_hidden = lax.dot_general(
            grad_block, down_matrix, (((1,), (1,)), ((), ())), preferred_element_type=jnp.float32
        )
        grad_gate = (
            grad_hidden * up_value * sigmoid_gate * (1.0 + gate_value * (1.0 - sigmoid_gate)) * live
        ).astype(jnp.bfloat16)
        grad_up = (grad_hidden * activated * live).astype(jnp.bfloat16)
        total_gate = add_into(total_gate, contract_rows(row_block, grad_gate), expert)
        total_up = add_into(total_up, contract_rows(row_block, grad_up), expert)
        total_down = add_into(total_down, contract_rows(hidden, grad_block), expert)
        return ((total_gate, total_up, total_down), None)

    totals, unused = lax.scan(
        step, (zeros_gate, zeros_gate, zeros_down), (row_blocks, grad_blocks, owner, alive)
    )
    return totals


def relocate(arrays, matching):
    groups = lax.axis_size("expert")
    joined = jnp.concatenate([array_piece.reshape(groups, -1) for array_piece in arrays], axis=1)
    spread = lax.all_to_all(joined, "expert", split_axis=0, concat_axis=0, tiled=True)
    ordered = jnp.take(spread, matching, axis=0)
    settled = lax.all_to_all(ordered, "expert", split_axis=0, concat_axis=0, tiled=True)
    pieces = []
    offset = 0
    for array_piece in arrays:
        length = array_piece.size // groups
        pieces.append(settled[:, offset : offset + length].reshape(array_piece.shape))
        offset = offset + length
    return pieces


def on_device_plain(tokens, grad_out, gate_weight, up_weight, down_weight, matching, block_counts):
    moved = relocate((gate_weight, up_weight, down_weight), matching)
    weight_gate, weight_up, weight_down = (
        lax.all_gather(moved[0], "dp", axis=1, tiled=True),
        lax.all_gather(moved[1], "dp", axis=1, tiled=True),
        lax.all_gather(moved[2], "dp", axis=2, tiled=True),
    )
    rows_full, grads_full = (
        lax.all_gather(tokens[0, 0], "hidden", axis=1, tiled=True),
        lax.all_gather(grad_out[0, 0], "hidden", axis=1, tiled=True),
    )
    blocks = rows_full.shape[0] // BLOCK
    width = rows_full.shape[1]
    owner, alive = block_owners(block_counts[0, 0], blocks)
    totals = expert_terms(
        rows_full.reshape(blocks, BLOCK, width),
        grads_full.reshape(blocks, BLOCK, width),
        weight_gate,
        weight_up,
        weight_down,
        owner,
        alive,
    )
    summed = (
        lax.psum_scatter(
            totals[0].astype(jnp.bfloat16), "dp", scatter_dimension=1, tiled=True
        ).astype(jnp.float32),
        lax.psum_scatter(
            totals[1].astype(jnp.bfloat16), "dp", scatter_dimension=1, tiled=True
        ).astype(jnp.float32),
        lax.psum_scatter(
            totals[2].astype(jnp.bfloat16), "dp", scatter_dimension=2, tiled=True
        ).astype(jnp.float32),
    )
    return (
        summed[0].astype(jnp.bfloat16),
        summed[1].astype(jnp.bfloat16),
        summed[2].astype(jnp.bfloat16),
    )


MESH = pl.DeviceIdType.MESH
TILE = 256


def flip(index, bit):
    return index + bit - 2 * bit * ((index // bit) % 2)


def fused_kernel(
    exchange, experts, counts_ref, match_ref, tok_ref, grad_ref, gate_ref, up_ref, down_ref,
    out_gate, out_up, out_down,
    tok_all, grad_all, gu_all, dn_all, own_gate, own_up, own_down, old_gate, old_up, old_down,
    acc_gu, acc_gh, pre, hid, gate_sel, up_sel,
    part_gu, part_dn, core_gu, core_dn, sum_gu, sum_dn, far_gu, far_dn,
    dn_end, hid_out, hid_in, hid_end, acc_end, gh_out, gh_in,
    part_de, core_de, sum_de, far_de, done_de, got_de,
    z_send, z_recv, y_send, y_recv, w_send, w_recv, r_send, r_recv, e_send, e_recv, l_sem,
):
    zs = lax.axis_size("hidden")
    h = lax.axis_index("hidden")
    d = lax.axis_index("dp")
    p = lax.axis_index("expert")
    rows, feats = tok_ref.shape
    width = gate_ref.shape[2]
    blocks = rows // BLOCK
    near, far = flip(d, 1), flip(d, 2)
    cross = flip(near, 2)
    middle = (h > 0) & (h < zs - 1)
    border = (h == 0) | (h == zs - 1)
    helper = 1 + (h // (zs - 1)) * (zs - 3)
    end = (h - 1) * (zs - 1)
    last = (zs - 2 - h) * (zs - 1)

    def remote(source, target, send, recv, where):
        return pltpu.make_async_remote_copy(
            src_ref=source, dst_ref=target, send_sem=send, recv_sem=recv,
            device_id=where, device_id_type=MESH,
        )

    barrier = pltpu.get_barrier_semaphore()
    for bit_partner in (near, far):
        pl.semaphore_signal(barrier, inc=1, device_id={"dp": bit_partner}, device_id_type=MESH)
    if exchange:
        pl.semaphore_signal(barrier, inc=1, device_id={"expert": 1 - p}, device_id_type=MESH)

    @pl.when(h > 0)
    def _():
        pl.semaphore_signal(barrier, inc=1, device_id={"hidden": h - 1}, device_id_type=MESH)

    @pl.when(h < zs - 1)
    def _():
        pl.semaphore_signal(barrier, inc=1, device_id={"hidden": h + 1}, device_id_type=MESH)

    peers = (h + zs - 1) // zs + (2 * zs - 2 - h) // zs
    pl.semaphore_wait(barrier, peers + (3 if exchange else 2))

    mine = (tok_ref, grad_ref)
    whole = (tok_all, grad_all)

    def line(kind, way, step, slab):
        to = h + 1 if way == 0 else h - 1
        source = mine[kind] if step == 0 else whole[kind].at[slab]
        return remote(
            source, whole[kind].at[slab], z_send.at[kind, way, step], z_recv.at[kind, way, step],
            {"hidden": to},
        )

    def sends(kind, way, step):
        if way == 0:
            return (h + 1 < zs - kind) & (h - step >= 0), h - step
        return (h - 1 >= kind) & (h + step < zs), h + step

    def takes(kind, way, step):
        if way == 0:
            valid, slab = h - 1 - step >= 0, h - 1 - step
        else:
            valid, slab = h + 1 + step < zs, h + 1 + step
        return (valid & middle) if kind else valid, slab

    def line_start(kind, step, ways=(0, 1)):
        for way in ways:
            valid, slab = sends(kind, way, step)

            @pl.when(valid)
            def _():
                line(kind, way, step, slab).start()

    def line_finish(kind, step):
        for way in (0, 1):
            valid, slab = sends(kind, way, step)

            @pl.when(valid)
            def _():
                line(kind, way, step, slab).wait_send()

    def line_take(kind, step, ways=(0, 1)):
        for way in ways:
            valid, slab = takes(kind, way, step)

            @pl.when(valid)
            def _():
                line(kind, way, step, slab).wait_recv()
        if step + 1 < zs - 1:
            line_start(kind, step + 1, ways)

    def swap(i):
        source = (gate_ref, up_ref, down_ref)[i]
        target = (old_gate, old_up, old_down)[i]
        return remote(source, target, y_send.at[i], y_recv.at[i], {"expert": 1 - p})

    line_start(0, 0)
    if exchange:
        for i in range(3):
            swap(i).start()
    local = [
        pltpu.make_async_copy(source, target, l_sem.at[i])
        for i, (source, target) in enumerate((
            (gate_ref, own_gate), (up_ref, own_up), (down_ref, own_down),
            (tok_ref, tok_all.at[h]), (grad_ref, grad_all.at[h]),
        ))
    ]
    for copy in local:
        copy.start()

    def chosen(own, other, e):
        if not exchange:
            return own[e]
        return jnp.where(match_ref[p] == p, own[e], other[e])

    weights = (gu_all, dn_all)

    def spread(kind, i):
        slab = (d, d, far)[i]
        to = (far, near, near)[i]
        ref = weights[kind].at[slab]
        return remote(ref, ref, w_send.at[kind, i], w_recv.at[kind, i], {"dp": to})

    def arrived(kind, i):
        slab = (far, near, cross)[i]
        ref = weights[kind].at[slab]
        remote(ref, ref, w_send.at[kind, i], w_recv.at[kind, i], {"dp": near}).wait_recv()

    line_take(0, 0)
    line_start(1, 0)
    for copy in local:
        copy.wait()
    if exchange:
        swap(0).wait_recv()
        swap(1).wait_recv()
    for e in range(experts):
        gu_all[d, e, :, :width] = chosen(own_gate, old_gate, e)
        gu_all[d, e, :, width:] = chosen(own_up, old_up, e)
    spread(0, 0).start()
    spread(0, 1).start()
    if exchange:
        swap(2).wait_recv()
    for e in range(experts):
        dn_all[d, e * width : (e + 1) * width, :] = chosen(own_down, old_down, e)
    spread(1, 0).start()
    spread(1, 1).start()
    line_take(0, 1)

    @pl.when(h == 1)
    def _():
        line(1, 0, 0, h - 1).wait_recv()
        line(1, 0, 1, h - 1).start()

    @pl.when(h == zs - 2)
    def _():
        line(1, 1, 0, h + 1).wait_recv()
        line(1, 1, 1, h + 1).start()

    for kind in (0, 1):
        arrived(kind, 0)
        spread(kind, 2).start()
    for kind in (0, 1):
        arrived(kind, 1)
        arrived(kind, 2)

    def lend(i, owner, to):
        slab = owner + (i + 1) * (1 - 2 * (owner // (zs - 1)))
        return remote(
            dn_all.at[slab], dn_end.at[slab], e_send.at[i], e_recv.at[i], {"hidden": to}
        )

    hidden_out = remote(hid_out, hid_in, e_send.at[3], e_recv.at[3], {"hidden": helper})
    grads_out = remote(gh_out, gh_in, e_send.at[4], e_recv.at[4], {"hidden": end})
    down_out = remote(done_de, got_de, e_send.at[5], e_recv.at[5], {"hidden": end})

    @pl.when(border)
    def _():
        for i in range(3):
            lend(i, h, helper).start()

    def add_tokens(slab, first=False):
        @pl.loop(0, rows // TILE)
        def _(i):
            part = pl.ds(pl.multiple_of(i * TILE, TILE), TILE)
            for e in range(experts):
                term = jnp.dot(tok_all[slab, part], gu_all[slab, e], preferred_element_type=jnp.float32)
                acc_gu[e, part] = term if first else acc_gu[e, part] + term

    def add_grads(slab, first=False, total=acc_gh, weight=dn_all):
        @pl.loop(0, rows // TILE)
        def _(i):
            part = pl.ds(pl.multiple_of(i * TILE, TILE), TILE)
            term = lax.dot_general(
                grad_all[slab, part], weight[slab], (((1,), (1,)), ((), ())),
                preferred_element_type=jnp.float32,
            )
            total[part] = term if first else total[part] + term

    def add_step(step):
        for way in (0, 1):
            valid, slab = takes(0, way, step)

            @pl.when(valid)
            def _():
                add_tokens(slab)

    add_tokens(h, True)
    add_grads(h, True)
    add_step(0)
    add_step(1)
    line_take(0, zs - 2)
    add_step(zs - 2)

    bounds = [counts_ref[0]]
    for e in range(1, experts):
        bounds.append(bounds[-1] + counts_ref[e])
    picks, masks = [], []
    for b in range(blocks):
        owner = jnp.int32(0)
        for e in range(experts):
            owner = owner + jnp.where(b >= bounds[e], 1, 0)
        owner = jnp.minimum(owner, experts - 1)
        alive = jnp.where(b < bounds[-1], 1.0, 0.0)
        picks.append([jnp.where(owner == e, 1.0, 0.0) for e in range(experts)])
        masks.append([picks[b][e] * alive for e in range(experts)])

    for b in range(blocks):
        part = slice(b * BLOCK, (b + 1) * BLOCK)
        both = sum(acc_gu[e, part] * picks[b][e] for e in range(experts))
        gate_value, up_value = both[:, :width], both[:, width:]
        gate_sel[part] = gate_value
        up_sel[part] = up_value
        hidden = gate_value * jax.nn.sigmoid(gate_value) * up_value
        hid_out[part] = (hidden * sum(masks[b])).astype(jnp.bfloat16)
        for e in range(experts):
            hid[part, e * width : (e + 1) * width] = (hidden * masks[b][e]).astype(jnp.bfloat16)

    @pl.when(border)
    def _():
        hidden_out.start()

    parts = (part_gu, part_dn, part_de)
    cores = (core_gu, core_dn, core_de)
    sums = (sum_gu, sum_dn, sum_de)
    fars = (far_gu, far_dn, far_de)

    def reduce_near(kind, i):
        slab = (cross, near)[i]
        return remote(
            parts[kind].at[slab], cores[kind].at[i], r_send.at[kind, i], r_recv.at[kind, i],
            {"dp": near},
        )

    def reduce_far(kind):
        return remote(
            sums[kind], fars[kind], r_send.at[kind, 2], r_recv.at[kind, 2], {"dp": far}
        )

    def down_term(kind, slab):
        left = hid if kind == 1 else hid_end
        parts[kind][slab] = lax.dot_general(
            left[...], grad_all[slab], (((0,), (0,)), ((), ())), preferred_element_type=jnp.float32
        ).astype(jnp.bfloat16)

    def gate_term(slab):
        @pl.loop(0, feats // TILE)
        def _(i):
            part = pl.ds(pl.multiple_of(i * TILE, TILE), TILE)
            part_gu[slab, part] = lax.dot_general(
                tok_all[slab, :, part], pre[...], (((0,), (0,)), ((), ())),
                preferred_element_type=jnp.float32,
            ).astype(jnp.bfloat16)

    def add_near(kind, i, slab):
        return parts[kind][slab].astype(jnp.float32) + cores[kind][i].astype(jnp.float32)

    def down_phase(kind, late):
        def at_turn(slab):
            return pl.when(slab == last if late else slab != last)

        @at_turn(cross)
        def _():
            down_term(kind, cross)
            reduce_near(kind, 0).start()

        @at_turn(far)
        def _():
            down_term(kind, far)
            reduce_near(kind, 0).wait_recv()
            sums[kind][...] = add_near(kind, 0, far).astype(jnp.bfloat16)
            reduce_far(kind).start()

        @at_turn(near)
        def _():
            down_term(kind, near)
            reduce_near(kind, 1).start()

        @at_turn(d)
        def _():
            down_term(kind, d)

    @pl.when(middle)
    def _():
        @pl.when(h == 1)
        def _():
            line(1, 1, 0, h + 1).wait_recv()

        @pl.when(h == zs - 2)
        def _():
            line(1, 0, 0, h - 1).wait_recv()

        add_grads(h - 1)
        add_grads(h + 1)
        down_phase(1, False)
        for i in range(3):
            lend(i, end, helper).wait_recv()
        add_grads(h, True, acc_end, dn_end)
        add_grads(zs - 1 - h, False, acc_end, dn_end)
        hidden_out.wait_recv()
        for b in range(blocks):
            part = slice(b * BLOCK, (b + 1) * BLOCK)
            value = hid_in[part].astype(jnp.float32)
            for e in range(experts):
                hid_end[part, e * width : (e + 1) * width] = (value * masks[b][e]).astype(
                    jnp.bfloat16
                )
        down_phase(2, False)

        @pl.when(h == 1)
        def _():
            line(1, 1, 1, h + 2).wait_recv()

        @pl.when(h == zs - 2)
        def _():
            line(1, 0, 1, h - 2).wait_recv()

        add_grads(last, False, acc_end, dn_end)
        for b in range(blocks):
            part = slice(b * BLOCK, (b + 1) * BLOCK)
            gh_out[part] = sum(
                acc_end[part, e * width : (e + 1) * width] * picks[b][e] for e in range(experts)
            ).astype(jnp.bfloat16)
        grads_out.start()
        down_phase(2, True)
        add_grads(last)
        gh_in[...] = jnp.zeros_like(gh_in)

    @pl.when(border)
    def _():
        grads_out.wait_recv()

    for b in range(blocks):
        part = slice(b * BLOCK, (b + 1) * BLOCK)
        gate_value, up_value = gate_sel[part], up_sel[part]
        grad_hidden = sum(
            acc_gh[part, e * width : (e + 1) * width] * picks[b][e] for e in range(experts)
        ) + gh_in[part].astype(jnp.float32)
        s = jax.nn.sigmoid(gate_value)
        grad_gate = grad_hidden * up_value * s * (1.0 + gate_value * (1.0 - s))
        grad_up = grad_hidden * gate_value * s
        for e in range(experts):
            at = e * 2 * width
            pre[part, at : at + width] = (grad_gate * masks[b][e]).astype(jnp.bfloat16)
            pre[part, at + width : at + 2 * width] = (grad_up * masks[b][e]).astype(jnp.bfloat16)

    gate_term(cross)
    reduce_near(0, 0).start()
    gate_term(far)
    reduce_near(0, 0).wait_recv()
    sum_gu[...] = add_near(0, 0, far).astype(jnp.bfloat16)
    reduce_far(0).start()
    gate_term(near)
    reduce_near(0, 1).start()

    @pl.when(middle)
    def _():
        down_phase(1, True)

    gate_term(d)

    @pl.when(middle)
    def _():
        reduce_near(2, 1).wait_recv()
        reduce_far(2).wait_recv()
        total = add_near(2, 1, d) + far_de[...].astype(jnp.float32)
        done_de[...] = total.astype(jnp.bfloat16)
        down_out.start()

    reduce_near(0, 1).wait_recv()
    reduce_far(0).wait_recv()
    total = add_near(0, 1, d) + far_gu[...].astype(jnp.float32)
    for e in range(experts):
        at = e * 2 * width
        out_gate[e] = total[:, at : at + width].astype(jnp.bfloat16)
        out_up[e] = total[:, at + width : at + 2 * width].astype(jnp.bfloat16)

    @pl.when(middle)
    def _():
        reduce_near(1, 1).wait_recv()
        reduce_far(1).wait_recv()
        total = add_near(1, 1, d) + far_dn[...].astype(jnp.float32)
        for e in range(experts):
            out_down[e] = total[e * width : (e + 1) * width].astype(jnp.bfloat16)

    @pl.when(border)
    def _():
        down_out.wait_recv()
        for e in range(experts):
            out_down[e] = got_de[e * width : (e + 1) * width]

    def sent(kind):
        for i in range(2):
            reduce_near(kind, i).wait_send()
        reduce_far(kind).wait_send()

    for kind in (0, 1):
        for step in range(zs - 1):
            line_finish(kind, step)
        for i in range(3):
            spread(kind, i).wait_send()
    sent(0)

    @pl.when(middle)
    def _():
        sent(1)
        sent(2)
        grads_out.wait_send()
        down_out.wait_send()

    @pl.when(border)
    def _():
        for i in range(3):
            lend(i, h, helper).wait_send()
        hidden_out.wait_send()

    if exchange:
        for i in range(3):
            swap(i).wait_send()


def on_device_fused(tokens, grad_out, gate_weight, up_weight, down_weight, matching, block_counts):
    groups = lax.axis_size("expert")
    zs = lax.axis_size("hidden")
    ds = lax.axis_size("dp")
    exchange = groups == 2
    if not exchange:
        gate_weight, up_weight, down_weight = relocate(
            (gate_weight, up_weight, down_weight), matching
        )
        matching = jnp.zeros_like(matching)
    rows, feats = tokens.shape[2:]
    experts, part, width = gate_weight.shape
    vmem = pl.BlockSpec(memory_space=pltpu.VMEM)
    smem = pl.BlockSpec(memory_space=pltpu.SMEM)
    half, full = jnp.bfloat16, jnp.float32
    wide = experts * 2 * width
    tall = experts * width
    dma = pltpu.SemaphoreType.DMA
    return pl.pallas_call(
        functools.partial(fused_kernel, exchange, experts),
        out_shape=tuple(
            jax.ShapeDtypeStruct(w.shape, half) for w in (gate_weight, up_weight, down_weight)
        ),
        in_specs=[smem, smem] + [pl.BlockSpec(memory_space=pltpu.HBM)] * 5,
        out_specs=(vmem,) * 3,
        scratch_shapes=[
            pltpu.VMEM((zs, rows, feats), half),
            pltpu.VMEM((zs, rows, feats), half),
            pltpu.VMEM((ds, experts, part, 2 * width), half),
            pltpu.VMEM((ds, tall, part), half),
            pltpu.VMEM(gate_weight.shape, half),
            pltpu.VMEM(up_weight.shape, half),
            pltpu.VMEM(down_weight.shape, half),
            pltpu.VMEM(gate_weight.shape, half),
            pltpu.VMEM(up_weight.shape, half),
            pltpu.VMEM(down_weight.shape, half),
            pltpu.VMEM((experts, rows, 2 * width), full),
            pltpu.VMEM((rows, tall), full),
            pltpu.VMEM((rows, wide), half),
            pltpu.VMEM((rows, tall), half),
            pltpu.VMEM((rows, width), full),
            pltpu.VMEM((rows, width), full),
            pltpu.VMEM((ds, part, wide), half),
            pltpu.VMEM((ds, tall, part), half),
            pltpu.VMEM((2, part, wide), half),
            pltpu.VMEM((2, tall, part), half),
            pltpu.VMEM((part, wide), half),
            pltpu.VMEM((tall, part), half),
            pltpu.VMEM((part, wide), half),
            pltpu.VMEM((tall, part), half),
            pltpu.VMEM((ds, tall, part), half),
            pltpu.VMEM((rows, width), half),
            pltpu.VMEM((rows, width), half),
            pltpu.VMEM((rows, tall), half),
            pltpu.VMEM((rows, tall), full),
            pltpu.VMEM((rows, width), half),
            pltpu.VMEM((rows, width), half),
            pltpu.VMEM((ds, tall, part), half),
            pltpu.VMEM((2, tall, part), half),
            pltpu.VMEM((tall, part), half),
            pltpu.VMEM((tall, part), half),
            pltpu.VMEM((tall, part), half),
            pltpu.VMEM((tall, part), half),
            dma((2, 2, zs - 1)),
            dma((2, 2, zs - 1)),
            dma((3,)),
            dma((3,)),
            dma((2, 3)),
            dma((2, 3)),
            dma((3, 3)),
            dma((3, 3)),
            dma((6,)),
            dma((6,)),
            dma((5,)),
        ],
        compiler_params=pltpu.CompilerParams(
            collective_id=0, has_side_effects=True, vmem_limit_bytes=63 * 1024 * 1024
        ),
    )(
        block_counts.reshape(-1), matching, tokens.reshape(rows, feats),
        grad_out.reshape(rows, feats), gate_weight, up_weight, down_weight,
    )


def fused_fits(mesh):
    return mesh.shape["dp"] == 4 and mesh.shape["hidden"] == 4


def solution(mesh):
    on_device = on_device_fused if fused_fits(mesh) else on_device_plain
    in_specs = (
        P("expert", "dp", None, "hidden"),
        P("expert", "dp", None, "hidden"),
        P("expert", "dp", "hidden"),
        P("expert", "dp", "hidden"),
        P("expert", "hidden", "dp"),
        P(),
        P("expert", "dp", None),
    )
    out_specs = (
        P("expert", "dp", "hidden"),
        P("expert", "dp", "hidden"),
        P("expert", "hidden", "dp"),
    )
    return jax.shard_map(
        on_device, mesh=mesh, in_specs=in_specs, out_specs=out_specs, check_vma=False
    )
```
